512 devices in a mesh: member: 4 (over x), lat: 16 (over y, core), lon: 8 (over z).
Axes of the slice: x: 4, y: 8, z: 8, core: 2. Of those that a mesh axis runs over, the one named last changes fastest.
Arguments:
- fields: float32 [8, 32, 640, 1024], P('member', None, 'lat', 'lon'), may hold values from -6 to 6
- spectra: float32 [9, 513], replicated, may hold values from 0.3 to 1.5
- band_weights: float32 [9, 640, 5], P(None, 'lat'), may hold values from -2.5 to 2.5
- band_start: int32 [640], P('lat'), may hold values from 0 to 635, as said below
- depth_weights: float32 [32, 9], replicated, may hold values from -2 to 2
- mix_weights: float32 [32, 32], replicated, may hold values from -1 to 1
- target: float32 [32, 640, 1024], P('member', 'lat', 'lon'), may hold values from -6 to 6
Outputs:
- crps: float32 [32, 640, 1024], P('member', 'lat', 'lon')
The draws below stay inside these ranges and needn't reach their ends.
Inputs may be any that keep to these rules, and one draw needn't show every extreme that they name: For each output row o, band_start[o] lies between o - 5 and o + 5 - 5 + 1; both ends of that offset range occur.
All inputs are finite; a program needn't handle non-finite values.
Results may differ from the reference program's by a relative error of at most 0.0001.
Values sent between devices are 32-bit elements; how exact they have to be, the bound alone decides.
No kernel may reach another device: no remote copies, remote signals or barrier semaphores. Data moves between devices by JAX's collectives and lax.ppermute only.
A program may use at most 64 MiB of HBM per device.

```python
import math
import jax
import jax.numpy as jnp
from jax import lax

C = 32
NLON = 1024
KB = 9
BAND = 5
REACH = 5
M = 8
NLAT = 640
NF = 513


def draw_band_start(key, part):
    row_idx = jnp.arange(NLAT, dtype=jnp.int32)
    jitter = jax.random.randint(key, (NLAT,), 0, 2 * REACH - BAND + 2, dtype=jnp.int32)
    jitter = jnp.where(row_idx % 7 == 0, 0, jitter)
    jitter = jnp.where(row_idx % 7 == 3, 2 * REACH - BAND + 1, jitter)
    start_row = jnp.clip(row_idx - REACH + jitter, 0, NLAT - BAND)
    start_row = jnp.where(row_idx == NLAT - 1, NLAT - BAND, start_row)
    return start_row.astype(jnp.int32)


def block_scale(stream_key, dims, cuts, low, largest):
    loudness, own = 1.0, jax.random.fold_in(stream_key, 6)
    for axis_at, parts in cuts:
        steps = jnp.exp(jax.random.uniform(jax.random.fold_in(own, axis_at), (parts,), jnp.float32, low / len(cuts), largest / len(cuts)))
        loudness = loudness * jnp.repeat(steps, dims[axis_at] // parts).reshape([-1 if axis == axis_at else 1 for axis in range(len(dims))])
    return loudness


def normal_values(own_key, shape, scale, limit, shards=(), held_as=jnp.bfloat16):
    values = jax.random.normal(own_key, shape, jnp.float32) * scale
    if len(shards) > 0:
        values = block_scale(own_key, shape, shards, -0.22, 0.18) * values
    return jnp.clip(values, min=-limit, max=limit).astype(held_as)


def setup_inputs(seed: int = 0) -> dict:
    splits = jax.random.split(jax.random.key(seed), 8)
    return {
        "fields": normal_values(splits[0], (M, C, NLAT, NLON), 1.0, 6.0, ((0, 4), (2, 16), (3, 8)), jnp.float32),
        "spectra": jnp.clip(jnp.exp(jax.random.uniform(splits[1], (KB, NF), jnp.float32, math.log(0.3), math.log(1.5))), 0.3, 1.5),
        "band_weights": normal_values(splits[2], (KB, NLAT, BAND), BAND ** -0.5, 2.5, ((1, 16),), jnp.float32),
        "band_start": draw_band_start(jax.random.fold_in(splits[7], 71), 0),
        "depth_weights": normal_values(splits[4], (C, KB), KB ** -0.5, 2.0, (), jnp.float32),
        "mix_weights": normal_values(splits[5], (C, C), C ** -0.5, 1.0, (), jnp.float32),
        "target": normal_values(splits[6], (C, NLAT, NLON), 1.0, 6.0, ((0, 4), (1, 16), (2, 8)), jnp.float32),
    }


def pair_total(ensemble):
    def step(member_idx, acc_sum):
        picked = lax.dynamic_index_in_dim(ensemble, member_idx, 0, keepdims=True)
        return acc_sum + jnp.sum(jnp.abs(picked - ensemble), axis=0)

    start_sum = jnp.zeros(ensemble.shape[1:], jnp.float32)
    return lax.fori_loop(0, ensemble.shape[0], step, start_sum)


def reference(fields, spectra, band_weights, band_start, depth_weights, mix_weights, target):
    offsets = jnp.arange(BAND, dtype=jnp.int32)
    read_rows = band_start.astype(jnp.int32)[:, None] + offsets[None, :]

    def one_member(field):
        spectrum = jnp.fft.rfft(field, axis=-1)
        summed = jnp.zeros_like(spectrum)
        for basis_idx in range(KB):
            band_sum = jnp.zeros_like(spectrum)
            for offset_idx in range(BAND):
                band_sum = band_sum + band_weights[basis_idx, :, offset_idx][None, :, None] * spectrum[:, read_rows[:, offset_idx], :]
            summed = summed + depth_weights[:, basis_idx][:, None, None] * spectra[basis_idx][None, None, :] * band_sum
        smooth = jnp.fft.irfft(summed, n=NLON, axis=-1)
        mixed_out = jnp.einsum("dc,cal->dal", mix_weights, smooth, precision=lax.Precision.HIGHEST)
        return jax.nn.gelu(mixed_out, approximate=False)

    hidden = lax.map(one_member, fields)
    members = hidden.shape[0]
    skill_term = jnp.mean(jnp.abs(hidden - target[None]), axis=0)
    spread = pair_total(hidden)
    return skill_term - spread / (2.0 * members * members)
```

```python
import functools
import math

import jax
import jax.numpy as jnp
import ml_dtypes
import numpy as np
from jax import lax
from jax.experimental import pallas as pl
from jax.experimental.pallas import tpu as pltpu
from jax.sharding import PartitionSpec as P

PTS = 8
TILE = 128
LENGTH = PTS * TILE
ROWPAD = 64
HALO = 8
S2 = math.sqrt(0.5)


def slot_frequencies():
    f1 = np.arange(TILE)
    zero = np.where(f1 <= 64, 8 * f1, 8 * (f1 - 64))
    four = 8 * (f1 % 64) + 4
    parts = [zero, four]
    for f0 in (1, 2, 3):
        f = 8 * f1 + f0
        f = np.minimum(f, LENGTH - f)
        parts += [f, f]
    return np.concatenate(parts).astype(np.int32)


def slot_scales():
    scale = np.full((LENGTH,), 2.0 / LENGTH)
    scale[0] = 1.0 / LENGTH
    scale[64] = 1.0 / LENGTH
    return scale.astype(np.float32)


def dft_tables():
    r = np.arange(TILE)[:, None]
    f1 = np.arange(TILE)[None, :]

    def ang(f):
        return 2.0 * np.pi * ((r * f) % LENGTH) / LENGTH

    tabs = np.zeros((4, 256, 256))
    low = f1 <= 64
    fz = np.where(low, 8 * f1, 8 * (f1 - 64))
    tabs[0, :TILE, :TILE] = np.where(low, np.cos(ang(fz)), -np.sin(ang(fz)))
    ff = 8 * (f1 % 64) + 4
    tabs[0, TILE:, TILE:] = np.where(f1 < 64, np.cos(ang(ff)), -np.sin(ang(ff)))
    for f0 in (1, 2, 3):
        a = ang(8 * f1 + f0)
        c, s = np.cos(a), np.sin(a)
        tabs[f0, :TILE, :TILE] = c
        tabs[f0, TILE:, :TILE] = s
        tabs[f0, :TILE, TILE:] = -s
        tabs[f0, TILE:, TILE:] = c
    full = tabs.astype(np.float32)
    hi = full.astype(ml_dtypes.bfloat16)
    lo = (tabs - hi.astype(np.float64)).astype(ml_dtypes.bfloat16)
    return hi, lo


def split(x):
    hi = x.astype(jnp.bfloat16)
    lo = (x - hi.astype(jnp.float32)).astype(jnp.bfloat16)
    return hi, lo


def mm(a, b):
    return jnp.dot(a, b, preferred_element_type=jnp.float32)


def mm_t(a, b):
    return lax.dot_general(a, b, (((1,), (1,)), ((), ())), preferred_element_type=jnp.float32)


def dot3(x, t_hi, t_lo, op):
    hi, lo = split(x)
    return op(hi, t_hi) + op(lo, t_hi) + op(hi, t_lo)


def forward_kernel(x_ref, hi_ref, lo_ref, o_ref, top_ref, bot_ref, *, circles, rows):
    x = [x_ref[q] for q in range(PTS)]
    a = [x[q] + x[q + 4] for q in range(4)]
    b = [x[q] - x[q + 4] for q in range(4)]
    e, g = a[0] + a[2], a[1] + a[3]
    p, m = S2 * (b[1] + b[3]), S2 * (b[1] - b[3])
    pairs = [
        (e + g, e - g),
        (b[0] + m, -p - b[2]),
        (a[0] - a[2], a[3] - a[1]),
        (b[0] - m, b[2] - p),
    ]
    for i, pair in enumerate(pairs):
        z = dot3(jnp.concatenate(pair, axis=1), hi_ref[i], lo_ref[i], mm)
        z = z.reshape(circles, rows, 256)
        lanes = slice(256 * i, 256 * (i + 1))
        o_ref[:, :, lanes] = z
        top_ref[:, :, lanes] = z[:, :HALO]
        bot_ref[:, :, lanes] = z[:, rows - HALO :]


def inverse_kernel(x_ref, up_ref, dn_ref, sel_ref, fac_ref, hi_ref, lo_ref, o_ref, y_ref, *, circles, rows, own_vars, n_basis):
    s_hi, s_lo = split(sel_ref[...])
    lhs = jnp.concatenate([s_hi, s_lo, s_hi], axis=1)
    pad = jnp.zeros((ROWPAD - rows - 2 * HALO, 256), jnp.float32)
    v = []
    for i in range(4):
        lanes = slice(256 * i, 256 * (i + 1))
        for c in range(circles):
            ext = jnp.concatenate([x_ref[c, :, lanes], up_ref[c, :, lanes], dn_ref[c, :, lanes], pad], axis=0)
            hi, lo = split(ext)
            z = mm(lhs, jnp.concatenate([hi, hi, lo], axis=0))
            fac = fac_ref[c % own_vars, :, lanes]
            acc = fac[0:1] * z[:rows]
            for k in range(1, n_basis):
                acc = acc + fac[k : k + 1] * z[k * rows : (k + 1) * rows]
            y_ref[c * rows : (c + 1) * rows, :] = acc
        v.append(dot3(y_ref[...], hi_ref[i], lo_ref[i], mm_t))
    v0, v4 = v[0][:, :TILE], v[0][:, TILE:]
    v1r, v1i = v[1][:, :TILE], v[1][:, TILE:]
    v2r, v2i = v[2][:, :TILE], v[2][:, TILE:]
    v3r, v3i = v[3][:, :TILE], v[3][:, TILE:]
    s, d = v0 + v4, v0 - v4
    even = [s + v2r, d - v2i, s - v2r, d + v2i]
    dr, si = v1r - v3r, v1i + v3i
    odd = [v1r + v3r, S2 * (dr - si), v3i - v1i, S2 * (-dr - si)]
    for q in range(4):
        o_ref[q] = even[q] + odd[q]
        o_ref[q + 4] = even[q] - odd[q]


def mix_kernel(x_ref, mix_ref, o_ref, *, n_lon, members, own_vars, rows, group):
    variables = n_lon * own_vars
    m_hi, m_lo = split(mix_ref[...])
    for rb in range(rows // 8):
        part = slice(rb * 8, rb * 8 + 8)
        data = jnp.concatenate(
            [x_ref[:, m, :, part, :].reshape(variables * 8, TILE) for m in range(members)], axis=1
        )
        hi, lo = split(data)
        z = mm(m_hi, hi) + mm(m_hi, lo) + mm(m_lo, hi)
        h = 0.5 * z * (1.0 + lax.erf(z * S2))
        for m in range(members):
            o_ref[:, m, :, part, :] = h[:, m * TILE : (m + 1) * TILE].reshape(
                variables // group, group, 8, TILE
            )


def score_kernel(h_ref, t_ref, o_ref, *, total):
    h = [h_ref[m] for m in range(total)]
    t = t_ref[...]
    skill = jnp.abs(h[0] - t)
    for m in range(1, total):
        skill = skill + jnp.abs(h[m] - t)
    spread = None
    for i in range(total):
        for j in range(i):
            d = jnp.abs(h[i] - h[j])
            spread = d if spread is None else spread + d
    o_ref[...] = skill * (1.0 / total) - spread * (1.0 / (total * total))


def local(fields, spectra, band_weights, band_start, depth_weights, mix_weights, target):
    members, variables, rows, tile = fields.shape
    n_basis = spectra.shape[0]
    band_len = band_weights.shape[2]
    n_member = lax.axis_size("member")
    n_lon = lax.axis_size("lon")
    n_lat = lax.axis_size("lat")
    own_vars = variables // n_lon
    circles = members * own_vars
    group = variables // n_member
    f32 = jnp.float32

    send = fields.reshape(members, n_lon, own_vars, rows, tile).transpose(1, 0, 2, 3, 4)
    recv = lax.all_to_all(send, "lon", split_axis=0, concat_axis=0, tiled=True)

    hi_np, lo_np = dft_tables()
    hi, lo = jnp.asarray(hi_np), jnp.asarray(lo_np)

    local_start = band_start - lax.axis_index("lat") * rows
    read = local_start[:, None] + jnp.arange(band_len, dtype=jnp.int32)[None, :]
    pos = jnp.where(read < 0, rows + HALO + read, jnp.where(read < rows, read, read + HALO))
    cols = jnp.arange(ROWPAD, dtype=jnp.int32)
    sel = jnp.zeros((n_basis, rows, ROWPAD), f32)
    for j in range(band_len):
        sel = sel + jnp.where(pos[None, :, j, None] == cols, band_weights[:, :, j, None], 0.0)
    sel = sel.reshape(n_basis * rows, ROWPAD)

    freq = jnp.asarray(slot_frequencies())
    pick = (jnp.arange(spectra.shape[1], dtype=jnp.int32)[:, None] == freq[None, :]).astype(f32)
    spec = jnp.dot(spectra, pick, precision=lax.Precision.HIGHEST) * slot_scales()[None, :]
    depth = lax.dynamic_slice_in_dim(depth_weights, lax.axis_index("lon") * own_vars, own_vars, 0)
    factor = depth[:, :, None] * spec[None]

    kron = (
        mix_weights[:, None, :, None] * jnp.eye(8, dtype=f32)[None, :, None, :]
    ).reshape(variables * 8, variables * 8)

    flat = circles * rows
    x, top, bot = pl.pallas_call(
        functools.partial(forward_kernel, circles=circles, rows=rows),
        out_shape=(
            jax.ShapeDtypeStruct((circles, rows, LENGTH), f32),
            jax.ShapeDtypeStruct((circles, HALO, LENGTH), f32),
            jax.ShapeDtypeStruct((circles, HALO, LENGTH), f32),
        ),
        name="forward",
    )(recv.reshape(n_lon, flat, tile), hi, lo)

    up = [(i, i + 1) for i in range(n_lat - 1)]
    down = [(i + 1, i) for i in range(n_lat - 1)]
    before = lax.ppermute(bot, "lat", up)
    after = lax.ppermute(top, "lat", down)

    smooth = pl.pallas_call(
        functools.partial(inverse_kernel, circles=circles, rows=rows, own_vars=own_vars, n_basis=n_basis),
        out_shape=jax.ShapeDtypeStruct((n_lon, flat, tile), f32),
        scratch_shapes=[pltpu.VMEM((flat, 256), f32)],
        name="inverse",
    )(x, before, after, sel, factor, hi, lo)

    tiles = lax.all_to_all(
        smooth.reshape(n_lon, members, own_vars, rows, tile), "lon", split_axis=0, concat_axis=0, tiled=True
    )
    hidden = pl.pallas_call(
        functools.partial(
            mix_kernel, n_lon=n_lon, members=members, own_vars=own_vars, rows=rows, group=group
        ),
        out_shape=jax.ShapeDtypeStruct((n_member, members, group, rows, tile), f32),
        name="mix",
    )(tiles, kron)

    every = lax.all_to_all(hidden, "member", split_axis=0, concat_axis=0, tiled=True)
    total = n_member * members
    return pl.pallas_call(
        functools.partial(score_kernel, total=total),
        out_shape=jax.ShapeDtypeStruct(target.shape, f32),
        name="score",
    )(every.reshape(total, group, rows, tile), target)


def solution(mesh):
    in_specs = (
        P("member", None, "lat", "lon"),
        P(),
        P(None, "lat", None),
        P("lat"),
        P(),
        P(),
        P("member", "lat", "lon"),
    )
    out_specs = P("member", "lat", "lon")
    return jax.shard_map(local, mesh=mesh, in_specs=in_specs, out_specs=out_specs, check_vma=False)
```

```python
import functools
import math

import jax
import jax.numpy as jnp
import ml_dtypes
import numpy as np
from jax import lax
from jax.experimental import pallas as pl
from jax.experimental.pallas import tpu as pltpu
from jax.sharding import PartitionSpec as P


PTS = 8
TILE = 128
LENGTH = PTS * TILE
ROWPAD = 64
HALO = 8
S2 = math.sqrt(0.5)


def slot_frequencies():
    f1 = np.arange(TILE)
    zero = np.where(f1 <= 64, 8 * f1, 8 * (f1 - 64))
    four = 8 * (f1 % 64) + 4
    parts = [zero, four]
    for f0 in (1, 2, 3):
        f = 8 * f1 + f0
        f = np.minimum(f, LENGTH - f)
        parts += [f, f]
    return np.concatenate(parts).astype(np.int32)


def slot_scales():
    scale = np.full((LENGTH,), 2.0 / LENGTH)
    scale[0] = 1.0 / LENGTH
    scale[64] = 1.0 / LENGTH
    return scale.astype(np.float32)


def dft_tables():
    r = np.arange(TILE)[:, None]
    f1 = np.arange(TILE)[None, :]

    def ang(f):
        return 2.0 * np.pi * ((r * f) % LENGTH) / LENGTH

    tabs = np.zeros((4, 256, 256))
    low = f1 <= 64
    fz = np.where(low, 8 * f1, 8 * (f1 - 64))
    tabs[0, :TILE, :TILE] = np.where(low, np.cos(ang(fz)), -np.sin(ang(fz)))
    ff = 8 * (f1 % 64) + 4
    tabs[0, TILE:, TILE:] = np.where(f1 < 64, np.cos(ang(ff)), -np.sin(ang(ff)))
    for f0 in (1, 2, 3):
        a = ang(8 * f1 + f0)
        c, s = np.cos(a), np.sin(a)
        tabs[f0, :TILE, :TILE] = c
        tabs[f0, TILE:, :TILE] = s
        tabs[f0, :TILE, TILE:] = -s
        tabs[f0, TILE:, TILE:] = c
    full = tabs.astype(np.float32)
    hi = full.astype(ml_dtypes.bfloat16)
    lo = (tabs - hi.astype(np.float64)).astype(ml_dtypes.bfloat16)
    return hi, lo


def split(x):
    hi = x.astype(jnp.bfloat16)
    lo = (x - hi.astype(jnp.float32)).astype(jnp.bfloat16)
    return hi, lo


def mm(a, b):
    return jnp.dot(a, b, preferred_element_type=jnp.float32)


def mm_t(a, b):
    return lax.dot_general(a, b, (((1,), (1,)), ((), ())), preferred_element_type=jnp.float32)


def dot3(x, t_hi, t_lo, op):
    hi, lo = split(x)
    return op(hi, t_hi) + op(lo, t_hi) + op(hi, t_lo)


def analyse(x, hi_ref, lo_ref, store):
    a = [x[q] + x[q + 4] for q in range(4)]
    b = [x[q] - x[q + 4] for q in range(4)]
    e, g = a[0] + a[2], a[1] + a[3]
    p, m = S2 * (b[1] + b[3]), S2 * (b[1] - b[3])
    pairs = [
        (e + g, e - g),
        (b[0] + m, -p - b[2]),
        (a[0] - a[2], a[3] - a[1]),
        (b[0] - m, b[2] - p),
    ]
    for i, pair in enumerate(pairs):
        store(i, dot3(jnp.concatenate(pair, axis=1), hi_ref[i], lo_ref[i], mm))


def forward_kernel(x_ref, hi_ref, lo_ref, top_ref, mid_ref, bot_ref, *, circles, rows):
    def store(i, z):
        lanes = slice(256 * i, 256 * (i + 1))
        z = z.reshape(circles, rows, 256)
        top_ref[:, :, lanes] = z[:, :HALO]
        mid_ref[:, :, lanes] = z[:, HALO : rows - HALO]
        bot_ref[:, :, lanes] = z[:, rows - HALO :]

    analyse([x_ref[q] for q in range(PTS)], hi_ref, lo_ref, store)


def banded(ext, lhs, fac, count, n_basis):
    hi, lo = split(ext)
    z = mm(lhs, jnp.concatenate([hi, hi, lo], axis=0))
    acc = fac[0:1] * z[:count]
    for k in range(1, n_basis):
        acc = acc + fac[k : k + 1] * z[k * count : (k + 1) * count]
    return acc


def wide_selector(sel_ref):
    s_hi, s_lo = split(sel_ref[...])
    return jnp.concatenate([s_hi, s_lo, s_hi], axis=1)


def combine(v):
    v0, v4 = v[0][:, :TILE], v[0][:, TILE:]
    v1r, v1i = v[1][:, :TILE], v[1][:, TILE:]
    v2r, v2i = v[2][:, :TILE], v[2][:, TILE:]
    v3r, v3i = v[3][:, :TILE], v[3][:, TILE:]
    s, d = v0 + v4, v0 - v4
    even = [s + v2r, d - v2i, s - v2r, d + v2i]
    dr, si = v1r - v3r, v1i + v3i
    odd = [v1r + v3r, S2 * (dr - si), v3i - v1i, S2 * (-dr - si)]
    return [e + o for e, o in zip(even, odd)] + [e - o for e, o in zip(even, odd)]


def inner_kernel(
    top_ref, mid_ref, bot_ref, sel_ref, fac_ref, hi_ref, lo_ref, o_ref, near_ref, y_ref, *, own_vars, n_basis, parts
):
    circles, count, _ = mid_ref.shape
    near_ref[:, :HALO] = mid_ref[:, :HALO]
    near_ref[:, HALO:] = mid_ref[:, count - HALO :]
    lhs = wide_selector(sel_ref)
    span = 8 * circles
    pad = jnp.zeros((8, 256), jnp.float32)
    v = []
    for i in range(4):
        lanes = slice(256 * i, 256 * (i + 1))
        for mc in range(circles):
            ext = jnp.concatenate([top_ref[mc, :, lanes], mid_ref[mc, :, lanes], bot_ref[mc, :, lanes], pad], axis=0)
            acc = banded(ext, lhs, fac_ref[mc % own_vars, :, lanes], count, n_basis)
            for p in range(parts - 1):
                y_ref[p * span + 8 * mc : p * span + 8 * mc + 8, :] = acc[8 * p : 8 * p + 8]
        v.append(dot3(y_ref[...], hi_ref[i], lo_ref[i], mm_t))
    for q, piece in enumerate(combine(v)):
        for p in range(parts - 1):
            o_ref[p, q] = piece[p * span : (p + 1) * span]


def edge_kernel(
    top_ref, bot_ref, near_ref, up_ref, dn_ref, in_ref, sel_ref, fac_ref, hi_ref, lo_ref, o_ref, y_ref, *, members, own_vars, n_basis, parts, tail
):
    lhs = wide_selector(sel_ref)
    span = 8 * members * own_vars
    main, rest = 8 * own_vars, tail * own_vars
    v = []
    for i in range(4):
        lanes = slice(256 * i, 256 * (i + 1))
        for m in range(members):
            for c in range(own_vars):
                mc = m * own_vars + c
                ext = jnp.concatenate(
                    [ref[mc, :, lanes] for ref in (top_ref, near_ref, bot_ref, up_ref, dn_ref)], axis=0
                )
                acc = banded(ext, lhs, fac_ref[c, :, lanes], 16, n_basis)
                y_ref[8 * mc : 8 * mc + 8, :] = acc[:8]
                for p in range(parts):
                    lead = span + (p * members + m) * rest + tail * c
                    y_ref[lead : lead + tail, :] = acc[8 + tail * p : 8 + tail * (p + 1)]
        v.append(dot3(y_ref[...], hi_ref[i], lo_ref[i], mm_t))
    for q, piece in enumerate(combine(v)):
        for p in range(parts):
            for m in range(members):
                at = m * (main + rest)
                if p:
                    o_ref[p, q, at : at + main] = in_ref[p - 1, q, m * main : (m + 1) * main]
                else:
                    o_ref[p, q, at : at + main] = piece[m * main : (m + 1) * main]
                lead = span + (p * members + m) * rest
                o_ref[p, q, at + main : at + main + rest] = piece[lead : lead + rest]


def send_kernel(x_ref, o_ref, buf_ref, in_sem, out_sem, *, members, n_lon, own_vars):
    loads, stores = [], []
    for z in range(n_lon):
        for m in range(members):
            loads.append(
                pltpu.make_async_copy(
                    x_ref.at[m, pl.ds(z * own_vars, own_vars)],
                    buf_ref.at[z, pl.ds(m * own_vars, own_vars)],
                    in_sem.at[z * members + m],
                )
            )
        stores.append(pltpu.make_async_copy(buf_ref.at[z], o_ref.at[z], out_sem.at[z]))
    for copy in loads:
        copy.start()
    for z in range(n_lon):
        for m in range(members):
            loads[z * members + m].wait()
        stores[z].start()
    for copy in stores:
        copy.wait()


def mixed(x_ref, k_refs, members, own_vars, n_member, n_lon):
    block = x_ref.shape[2] // members
    main = 8 * own_vars
    k_hi, k_lo, r_hi, r_lo = [ref[...] for ref in k_refs]
    out = []
    for m in range(members):
        lead = m * block
        for j in range(0, n_member, 2):
            pair = range(j, min(j + 2, n_member))
            big = jnp.concatenate([x_ref[i, :, lead : lead + main, :].reshape(n_lon * main, TILE) for i in pair], axis=1)
            small = jnp.concatenate(
                [x_ref[i, :, lead + main : lead + block, :].reshape(n_lon * (block - main), TILE) for i in pair], axis=1
            )
            hi, lo = split(big)
            z = mm(k_hi, hi) + mm(k_hi, lo) + mm(k_lo, hi)
            hi, lo = split(small)
            y = mm(r_hi, hi) + mm(r_hi, lo) + mm(r_lo, hi)
            h = jnp.concatenate([z, y], axis=0)
            h = 0.5 * h * (1.0 + lax.erf(h * S2))
            for i in range(len(pair)):
                out.append(h[:, i * TILE : (i + 1) * TILE])
    return out


def score_kernel(*refs, total, main, parts, earlier, sizes):
    prior = refs[:earlier]
    x_ref, *k_refs, t_ref, o_ref, h_ref = refs[earlier:]
    ready = [(ref, i) for ref in prior for i in range(ref.shape[0])]
    for i, h in enumerate(mixed(x_ref, k_refs, **sizes)):
        h_ref[i] = h
        ready.append((h_ref, i))
    width = main // parts
    rest = t_ref.shape[1] - width
    for p in range(parts):
        for lo, n, at in ((p * width, width, 0), (main + p * rest, rest, width)):
            t = t_ref[p, at : at + n, :]
            h = [ref[i, lo : lo + n, :] for ref, i in ready]
            skill = jnp.abs(h[0] - t)
            for m in range(1, total):
                skill = skill + jnp.abs(h[m] - t)
            spread = None
            for i in range(total):
                for j in range(i):
                    d = jnp.abs(h[i] - h[j])
                    spread = d if spread is None else spread + d
            o_ref[p, at : at + n, :] = skill * (1.0 / total) - spread * (1.0 / (total * total))


def spread_rows(t_ref, o_ref, parts, tail):
    group = t_ref.shape[0]
    for p in range(parts):
        for d in range(group):
            o_ref[p, 8 * d : 8 * d + 8, :] = t_ref[d, 8 * p : 8 * p + 8, :]
            lead = 8 * group + tail * d
            row = 8 * parts + tail * p
            o_ref[p, lead : lead + tail, :] = t_ref[d, row : row + tail, :]


def join_rows_kernel(x_ref, o_ref, *, parts, tail):
    group = o_ref.shape[0]
    for p in range(parts):
        for d in range(group):
            o_ref[d, 8 * p : 8 * p + 8, :] = x_ref[p, 8 * d : 8 * d + 8, :]
            lead = 8 * group + tail * d
            row = 8 * parts + tail * p
            o_ref[d, row : row + tail, :] = x_ref[p, lead : lead + tail, :]


def expand(mix, n):
    size = mix.shape[0]
    span = size * n
    rep = lax.broadcasted_iota(jnp.int32, (span, size), 0) // n == lax.broadcasted_iota(jnp.int32, (span, size), 1)
    rep = rep.astype(jnp.float32).astype(jnp.bfloat16)
    row = lax.broadcasted_iota(jnp.int32, (span, span), 0) % n
    col = lax.broadcasted_iota(jnp.int32, (span, span), 1) % n
    full = []
    for part in split(mix):
        tall = mm(rep, part).astype(jnp.bfloat16)
        full.append(jnp.where(row == col, mm_t(tall, rep), 0.0).astype(jnp.bfloat16))
    return full


def prepare_kernel(mix_ref, t_ref, khi_ref, klo_ref, rhi_ref, rlo_ref, o_ref, *, parts, tail):
    khi_ref[...], klo_ref[...] = expand(mix_ref[...], 8)
    rhi_ref[...], rlo_ref[...] = expand(mix_ref[...], tail)
    spread_rows(t_ref, o_ref, parts, tail)


def in_vmem(*arrays):
    return [pltpu.with_memory_space_constraint(a, pltpu.VMEM) for a in arrays]


def block(fields, spectra, band_weights, band_start, depth_weights, mix_weights, target):
    members, variables, rows, tile = fields.shape
    n_basis = spectra.shape[0]
    band_len = band_weights.shape[2]
    n_member = lax.axis_size("member")
    n_lon = lax.axis_size("lon")
    n_lat = lax.axis_size("lat")
    own_vars = variables // n_lon
    group = variables // n_member
    parts = n_member
    tail = (rows - 8 * parts) // parts
    circles = members * own_vars
    f32 = jnp.float32
    vmem = pl.BlockSpec(memory_space=pltpu.VMEM)
    shape = jax.ShapeDtypeStruct

    hbm = pl.BlockSpec(memory_space=pl.ANY)
    send = pl.pallas_call(
        functools.partial(send_kernel, members=members, n_lon=n_lon, own_vars=own_vars),
        out_shape=shape((n_lon, circles, rows, tile), f32),
        in_specs=[hbm],
        out_specs=hbm,
        scratch_shapes=[
            pltpu.VMEM((n_lon, circles, rows, tile), f32),
            pltpu.SemaphoreType.DMA((members * n_lon,)),
            pltpu.SemaphoreType.DMA((n_lon,)),
        ],
        name="send",
    )(fields)
    received = lax.all_to_all(send, "lon", split_axis=0, concat_axis=0, tiled=True)

    width = group * (8 + tail)
    *krons, mine = pl.pallas_call(
        functools.partial(prepare_kernel, parts=parts, tail=tail),
        out_shape=(
            shape((variables * 8, variables * 8), jnp.bfloat16),
            shape((variables * 8, variables * 8), jnp.bfloat16),
            shape((variables * tail, variables * tail), jnp.bfloat16),
            shape((variables * tail, variables * tail), jnp.bfloat16),
            shape((parts, width, tile), f32),
        ),
        name="prepare",
    )(mix_weights, target)
    x_at = lax.axis_index("member")
    wanted = jnp.zeros((parts, width, tile), f32)
    own = lax.dynamic_index_in_dim(mine, x_at, 0, keepdims=True)
    wanted = lax.dynamic_update_slice_in_dim(wanted, own, x_at, 0)
    for s in range(1, n_member):
        ring = [(i, (i + s) % n_member) for i in range(n_member)]
        out = lax.dynamic_index_in_dim(mine, (x_at + s) % n_member, 0, keepdims=True)
        got = lax.ppermute(out, "member", ring)
        wanted = lax.dynamic_update_slice_in_dim(wanted, got, (x_at - s) % n_member, 0)

    hi_np, lo_np = dft_tables()
    hi, lo = jnp.asarray(hi_np), jnp.asarray(lo_np)

    local_start = band_start - lax.axis_index("lat") * rows
    read = local_start[:, None] + jnp.arange(band_len, dtype=jnp.int32)[None, :]
    pos = jnp.where(read < 0, rows + HALO + read, jnp.where(read < rows, read, read + HALO))
    cols = jnp.arange(ROWPAD, dtype=jnp.int32)
    sel = jnp.zeros((n_basis, rows, ROWPAD), f32)
    for j in range(band_len):
        sel = sel + jnp.where(pos[None, :, j, None] == cols, band_weights[:, :, j, None], 0.0)
    inner_sel = sel[:, 8 : rows - 8, : rows + 8].reshape(n_basis * (rows - 16), rows + 8)
    edge_sel = jnp.concatenate([sel[:, :8], sel[:, rows - 8 :]], axis=1)
    edge_sel = jnp.concatenate([edge_sel[:, :, :16], edge_sel[:, :, rows - 16 : rows + 16]], axis=2)
    edge_sel = edge_sel.reshape(n_basis * 16, 48)

    freq = jnp.asarray(slot_frequencies())
    pick = (jnp.arange(spectra.shape[1], dtype=jnp.int32)[:, None] == freq[None, :]).astype(f32)
    spec = jnp.dot(spectra, pick, precision=lax.Precision.HIGHEST) * slot_scales()[None, :]
    depth = lax.dynamic_slice_in_dim(depth_weights, lax.axis_index("lon") * own_vars, own_vars, 0)
    factor = depth[:, :, None] * spec[None]
    received, krons, wanted, inner_sel, edge_sel, factor = lax.optimization_barrier(
        (received, krons, wanted, inner_sel, edge_sel, factor)
    )

    up = [(i, i + 1) for i in range(n_lat - 1)]
    down = [(i + 1, i) for i in range(n_lat - 1)]
    top, mid, bot = pl.pallas_call(
        functools.partial(forward_kernel, circles=circles, rows=rows),
        out_shape=(
            shape((circles, HALO, LENGTH), f32),
            shape((circles, rows - 2 * HALO, LENGTH), f32),
            shape((circles, HALO, LENGTH), f32),
        ),
        in_specs=[vmem] * 3,
        name="forward",
    )(*in_vmem(received.reshape(n_lon, circles * rows, tile)), hi, lo)
    before = lax.ppermute(bot, "lat", up)
    after = lax.ppermute(top, "lat", down)
    inner, near = pl.pallas_call(
        functools.partial(inner_kernel, own_vars=own_vars, n_basis=n_basis, parts=parts),
        out_shape=(
            pltpu.VMEM((parts - 1, n_lon, 8 * circles, tile), f32),
            pltpu.VMEM((circles, 2 * HALO, LENGTH), f32),
        ),
        in_specs=[vmem] * 7,
        out_specs=(vmem, vmem),
        scratch_shapes=[pltpu.VMEM((8 * (parts - 1) * circles, 256), f32)],
        name="inner",
    )(top, mid, bot, inner_sel, factor, hi, lo)
    smooth = pl.pallas_call(
        functools.partial(
            edge_kernel, members=members, own_vars=own_vars, n_basis=n_basis, parts=parts, tail=tail
        ),
        out_shape=shape((parts, n_lon, circles * (8 + tail), tile), f32),
        in_specs=[vmem] * 10,
        scratch_shapes=[pltpu.VMEM((circles * (8 + parts * tail), 256), f32)],
        name="edge",
    )(top, bot, *in_vmem(near, before, after, inner), edge_sel, factor, hi, lo)
    moved = lax.all_to_all(
        smooth.reshape(parts * n_lon, *smooth.shape[2:]),
        ("member", "lon"),
        split_axis=0,
        concat_axis=0,
        tiled=True,
    ).reshape(smooth.shape)

    sizes = dict(members=members, own_vars=own_vars, n_member=n_member, n_lon=n_lon)
    height = variables * (8 + tail)
    total = n_member * members
    scored = pl.pallas_call(
        functools.partial(
            score_kernel, total=total, main=variables * 8, parts=parts, earlier=0, sizes=sizes
        ),
        out_shape=shape((parts, width, tile), f32),
        in_specs=[vmem] * 6,
        scratch_shapes=[pltpu.VMEM((total, height, tile), f32)],
        name="score",
    )(*in_vmem(moved), *krons, *in_vmem(wanted))
    back = lax.all_to_all(scored, "member", split_axis=0, concat_axis=0, tiled=True)
    return pl.pallas_call(
        functools.partial(join_rows_kernel, parts=parts, tail=tail),
        out_shape=shape(target.shape, f32),
        in_specs=[vmem],
        name="join_rows",
    )(*in_vmem(back))


def solution(mesh):
    in_specs = (
        P("member", None, "lat", "lon"),
        P(),
        P(None, "lat", None),
        P("lat"),
        P(),
        P(),
        P("member", "lat", "lon"),
    )
    out_specs = P("member", "lat", "lon")
    return jax.shard_map(block, mesh=mesh, in_specs=in_specs, out_specs=out_specs, check_vma=False)
```

```python
import functools
import math

import jax
import jax.numpy as jnp
import ml_dtypes
import numpy as np
from jax import lax
from jax.experimental import pallas as pl
from jax.experimental.pallas import tpu as pltpu
from jax.sharding import PartitionSpec as P


PTS = 8
TILE = 128
LENGTH = PTS * TILE
HALO = 8
REACH = 5
GRANT = pltpu.CompilerParams(vmem_limit_bytes=12 << 20)
S2 = math.sqrt(0.5)


def slot_frequencies():
    f1 = np.arange(TILE)
    zero = np.where(f1 <= 64, 8 * f1, 8 * (f1 - 64))
    parts = [zero, 8 * (f1 % 64) + 4]
    for f0 in (1, 2, 3):
        f = 8 * f1 + f0
        parts.append(np.minimum(f, LENGTH - f))
    return np.concatenate(parts).astype(np.int32)


def slot_scales():
    scale = np.full((5 * TILE,), 2.0 / LENGTH)
    scale[0] = 1.0 / LENGTH
    scale[64] = 1.0 / LENGTH
    return scale.astype(np.float32)


def dft_tables():
    r = np.arange(TILE)[:, None]
    f1 = np.arange(TILE)[None, :]

    def ang(f):
        return 2.0 * np.pi * ((r * f) % LENGTH) / LENGTH

    tabs = np.zeros((4, 256, 256))
    low = f1 <= 64
    fz = np.where(low, 8 * f1, 8 * (f1 - 64))
    tabs[0, :TILE, :TILE] = np.where(low, np.cos(ang(fz)), -np.sin(ang(fz)))
    ff = 8 * (f1 % 64) + 4
    tabs[0, TILE:, TILE:] = np.where(f1 < 64, np.cos(ang(ff)), -np.sin(ang(ff)))
    for f0 in (1, 2, 3):
        a = ang(8 * f1 + f0)
        c, s = np.cos(a), np.sin(a)
        tabs[f0, :TILE, :TILE] = c
        tabs[f0, TILE:, :TILE] = s
        tabs[f0, :TILE, TILE:] = -s
        tabs[f0, TILE:, TILE:] = c
    full = tabs.astype(np.float32)
    hi = full.astype(ml_dtypes.bfloat16)
    lo = (tabs - hi.astype(np.float64)).astype(ml_dtypes.bfloat16)
    return hi, lo


def split(x):
    hi = x.astype(jnp.bfloat16)
    lo = (x - hi.astype(jnp.float32)).astype(jnp.bfloat16)
    return hi, lo


def mm(a, b):
    return jnp.dot(a, b, preferred_element_type=jnp.float32)


def mm_t(a, b):
    return lax.dot_general(a, b, (((1,), (1,)), ((), ())), preferred_element_type=jnp.float32)


def dot3(x, t_hi, t_lo, op):
    hi, lo = split(x)
    both = op(jnp.concatenate([hi, lo], axis=0), t_hi)
    size = x.shape[0]
    return both[:size] + both[size:] + op(hi, t_lo)


def analyse(x, hi_ref, lo_ref, store):
    a = [x[q] + x[q + 4] for q in range(4)]
    b = [x[q] - x[q + 4] for q in range(4)]
    e, g = a[0] + a[2], a[1] + a[3]
    p, m = S2 * (b[1] + b[3]), S2 * (b[1] - b[3])
    pairs = [
        (e + g, e - g),
        (b[0] + m, -p - b[2]),
        (a[0] - a[2], a[3] - a[1]),
        (b[0] - m, b[2] - p),
    ]
    for i, pair in enumerate(pairs):
        store(i, dot3(jnp.concatenate(pair, axis=1), hi_ref[i], lo_ref[i], mm))


def forward_kernel(x_ref, hi_ref, lo_ref, top_ref, mid_ref, bot_ref, *, circles, rows):
    def store(i, z):
        lanes = slice(256 * i, 256 * (i + 1))
        z = z.reshape(circles, rows, 256)
        top_ref[:, :, lanes] = z[:, :HALO]
        mid_ref[:, :, lanes] = z[:, HALO : rows - HALO]
        bot_ref[:, :, lanes] = z[:, rows - HALO :]

    analyse([x_ref[q] for q in range(PTS)], hi_ref, lo_ref, store)


def shifted_sum(ext, coef_ref, c, at, count, lanes):
    acc = None
    for e in range(2 * REACH + 1):
        w = coef_ref[e, c, at : at + count, lanes]
        if w.shape[1] < ext.shape[1]:
            w = jnp.concatenate([w, w], axis=1)
        lead = HALO - REACH + e
        term = w * ext[lead : lead + count]
        acc = term if acc is None else acc + term
    return acc


def coef_lanes(i):
    return slice(0, 256) if i == 0 else slice(TILE * (i + 1), TILE * (i + 2))


def combine(v):
    v0, v4 = v[0][:, :TILE], v[0][:, TILE:]
    v1r, v1i = v[1][:, :TILE], v[1][:, TILE:]
    v2r, v2i = v[2][:, :TILE], v[2][:, TILE:]
    v3r, v3i = v[3][:, :TILE], v[3][:, TILE:]
    s, d = v0 + v4, v0 - v4
    even = [s + v2r, d - v2i, s - v2r, d + v2i]
    dr, si = v1r - v3r, v1i + v3i
    odd = [v1r + v3r, S2 * (dr - si), v3i - v1i, S2 * (-dr - si)]
    return [e + o for e, o in zip(even, odd)] + [e - o for e, o in zip(even, odd)]


def inner_kernel(
    top_ref, mid_ref, bot_ref, coef_ref, hi_ref, lo_ref, o_ref, near_ref, y_ref, *, own_vars, parts
):
    circles, count, _ = mid_ref.shape
    near_ref[:, :HALO] = mid_ref[:, :HALO]
    near_ref[:, HALO:] = mid_ref[:, count - HALO :]
    span = 8 * circles
    v = []
    for i in range(4):
        lanes = slice(256 * i, 256 * (i + 1))
        for mc in range(circles):
            ext = jnp.concatenate([top_ref[mc, :, lanes], mid_ref[mc, :, lanes], bot_ref[mc, :, lanes]], axis=0)
            acc = shifted_sum(ext, coef_ref, mc % own_vars, 0, count, coef_lanes(i))
            for p in range(parts - 1):
                y_ref[p * span + 8 * mc : p * span + 8 * mc + 8, :] = acc[8 * p : 8 * p + 8]
        v.append(dot3(y_ref[...], hi_ref[i], lo_ref[i], mm_t))
    for q, piece in enumerate(combine(v)):
        for p in range(parts - 1):
            o_ref[p, q] = piece[p * span : (p + 1) * span]


def edge_kernel(
    top_ref, bot_ref, near_ref, up_ref, dn_ref, in_ref, coef_ref, hi_ref, lo_ref, o_ref, y_ref, *, members, own_vars, parts, tail
):
    span = 8 * members * own_vars
    main, rest = 8 * own_vars, tail * own_vars
    v = []
    for i in range(4):
        lanes = slice(256 * i, 256 * (i + 1))
        for m in range(members):
            for c in range(own_vars):
                mc = m * own_vars + c
                first = jnp.concatenate([up_ref[mc, :, lanes], top_ref[mc, :, lanes], near_ref[mc, :HALO, lanes]], axis=0)
                final = jnp.concatenate([near_ref[mc, HALO:, lanes], bot_ref[mc, :, lanes], dn_ref[mc, :, lanes]], axis=0)
                y_ref[8 * mc : 8 * mc + 8, :] = shifted_sum(first, coef_ref, c, 0, 8, coef_lanes(i))
                last = shifted_sum(final, coef_ref, c, 8, 8, coef_lanes(i))
                for p in range(parts):
                    lead = span + (p * members + m) * rest + tail * c
                    y_ref[lead : lead + tail, :] = last[tail * p : tail * (p + 1)]
        v.append(dot3(y_ref[...], hi_ref[i], lo_ref[i], mm_t))
    for q, piece in enumerate(combine(v)):
        for p in range(parts):
            for m in range(members):
                at = m * (main + rest)
                if p:
                    o_ref[p, q, at : at + main] = in_ref[p - 1, q, m * main : (m + 1) * main]
                else:
                    o_ref[p, q, at : at + main] = piece[m * main : (m + 1) * main]
                lead = span + (p * members + m) * rest
                o_ref[p, q, at + main : at + main + rest] = piece[lead : lead + rest]


def send_kernel(x_ref, o_ref, buf_ref, in_sem, out_sem, *, members, n_lon, own_vars):
    loads, stores = [], []
    for z in range(n_lon):
        for m in range(members):
            loads.append(
                pltpu.make_async_copy(
                    x_ref.at[m, pl.ds(z * own_vars, own_vars)],
                    buf_ref.at[z, pl.ds(m * own_vars, own_vars)],
                    in_sem.at[z * members + m],
                )
            )
        stores.append(pltpu.make_async_copy(buf_ref.at[z], o_ref.at[z], out_sem.at[z]))
    for copy in loads:
        copy.start()
    for z in range(n_lon):
        for m in range(members):
            loads[z * members + m].wait()
        stores[z].start()
    for copy in stores:
        copy.wait()


def mixed(x_ref, k_refs, members, own_vars, n_member, n_lon):
    block = x_ref.shape[2] // members
    main = 8 * own_vars
    k_hi, k_lo, r_hi, r_lo = [ref[...] for ref in k_refs]
    out = []
    for m in range(members):
        lead = m * block
        for j in range(0, n_member, 2):
            pair = range(j, min(j + 2, n_member))
            big = jnp.concatenate([x_ref[i, :, lead : lead + main, :].reshape(n_lon * main, TILE) for i in pair], axis=1)
            small = jnp.concatenate(
                [x_ref[i, :, lead + main : lead + block, :].reshape(n_lon * (block - main), TILE) for i in pair], axis=1
            )
            hi, lo = split(big)
            z = mm(k_hi, hi) + mm(k_hi, lo) + mm(k_lo, hi)
            hi, lo = split(small)
            y = mm(r_hi, hi) + mm(r_hi, lo) + mm(r_lo, hi)
            h = jnp.concatenate([z, y], axis=0)
            h = 0.5 * h * (1.0 + lax.erf(h * S2))
            for i in range(len(pair)):
                out.append(h[:, i * TILE : (i + 1) * TILE])
    return out


def score_kernel(*refs, total, main, parts, earlier, sizes):
    prior = refs[:earlier]
    x_ref, *k_refs, t_ref, o_ref, h_ref = refs[earlier:]
    ready = [(ref, i) for ref in prior for i in range(ref.shape[0])]
    for i, h in enumerate(mixed(x_ref, k_refs, **sizes)):
        h_ref[i] = h
        ready.append((h_ref, i))
    width = main // parts
    rest = t_ref.shape[1] - width
    for p in range(parts):
        for lo, n, at in ((p * width, width, 0), (main + p * rest, rest, width)):
            t = t_ref[p, at : at + n, :]
            h = [ref[i, lo : lo + n, :] for ref, i in ready]
            skill = jnp.abs(h[0] - t)
            for m in range(1, total):
                skill = skill + jnp.abs(h[m] - t)
            spread = None
            for i in range(total):
                for j in range(i):
                    d = jnp.abs(h[i] - h[j])
                    spread = d if spread is None else spread + d
            o_ref[p, at : at + n, :] = skill * (1.0 / total) - spread * (1.0 / (total * total))


def spread_rows(t_ref, o_ref, parts, tail):
    group = t_ref.shape[0]
    for p in range(parts):
        for d in range(group):
            o_ref[p, 8 * d : 8 * d + 8, :] = t_ref[d, 8 * p : 8 * p + 8, :]
            lead = 8 * group + tail * d
            row = 8 * parts + tail * p
            o_ref[p, lead : lead + tail, :] = t_ref[d, row : row + tail, :]


def join_rows_kernel(x_ref, o_ref, *, parts, tail):
    group = o_ref.shape[0]
    for p in range(parts):
        for d in range(group):
            o_ref[d, 8 * p : 8 * p + 8, :] = x_ref[p, 8 * d : 8 * d + 8, :]
            lead = 8 * group + tail * d
            row = 8 * parts + tail * p
            o_ref[d, row : row + tail, :] = x_ref[p, lead : lead + tail, :]


def expand(mix, n):
    size = mix.shape[0]
    span = size * n
    rep = lax.broadcasted_iota(jnp.int32, (span, size), 0) // n == lax.broadcasted_iota(jnp.int32, (span, size), 1)
    rep = rep.astype(jnp.float32).astype(jnp.bfloat16)
    row = lax.broadcasted_iota(jnp.int32, (span, span), 0) % n
    col = lax.broadcasted_iota(jnp.int32, (span, span), 1) % n
    full = []
    for part in split(mix):
        tall = mm(rep, part).astype(jnp.bfloat16)
        full.append(jnp.where(row == col, mm_t(tall, rep), 0.0).astype(jnp.bfloat16))
    return full


def prepare_kernel(mix_ref, t_ref, khi_ref, klo_ref, rhi_ref, rlo_ref, o_ref, *, parts, tail):
    khi_ref[...], klo_ref[...] = expand(mix_ref[...], 8)
    rhi_ref[...], rlo_ref[...] = expand(mix_ref[...], tail)
    spread_rows(t_ref, o_ref, parts, tail)


def in_vmem(*arrays):
    return [pltpu.with_memory_space_constraint(a, pltpu.VMEM) for a in arrays]


def block(fields, spectra, band_weights, band_start, depth_weights, mix_weights, target):
    members, variables, rows, tile = fields.shape
    n_basis = spectra.shape[0]
    band_len = band_weights.shape[2]
    n_member = lax.axis_size("member")
    n_lon = lax.axis_size("lon")
    n_lat = lax.axis_size("lat")
    own_vars = variables // n_lon
    group = variables // n_member
    parts = n_member
    tail = (rows - 8 * parts) // parts
    circles = members * own_vars
    f32 = jnp.float32
    vmem = pl.BlockSpec(memory_space=pltpu.VMEM)
    shape = jax.ShapeDtypeStruct

    hbm = pl.BlockSpec(memory_space=pl.ANY)
    send = pl.pallas_call(
        functools.partial(send_kernel, members=members, n_lon=n_lon, own_vars=own_vars),
        out_shape=shape((n_lon, circles, rows, tile), f32),
        in_specs=[hbm],
        out_specs=hbm,
        scratch_shapes=[
            pltpu.VMEM((n_lon, circles, rows, tile), f32),
            pltpu.SemaphoreType.DMA((members * n_lon,)),
            pltpu.SemaphoreType.DMA((n_lon,)),
        ],
        name="send",
        compiler_params=GRANT,
    )(pltpu.with_memory_space_constraint(fields, pltpu.HBM))
    received = lax.all_to_all(send, "lon", split_axis=0, concat_axis=0, tiled=True)

    width = group * (8 + tail)
    *krons, mine = pl.pallas_call(
        functools.partial(prepare_kernel, parts=parts, tail=tail),
        out_shape=(
            shape((variables * 8, variables * 8), jnp.bfloat16),
            shape((variables * 8, variables * 8), jnp.bfloat16),
            shape((variables * tail, variables * tail), jnp.bfloat16),
            shape((variables * tail, variables * tail), jnp.bfloat16),
            shape((parts, width, tile), f32),
        ),
        name="prepare",
    compiler_params=GRANT,
    )(mix_weights, target)
    x_at = lax.axis_index("member")
    wanted = jnp.zeros((parts, width, tile), f32)
    own = lax.dynamic_index_in_dim(mine, x_at, 0, keepdims=True)
    wanted = lax.dynamic_update_slice_in_dim(wanted, own, x_at, 0)
    for s in range(1, n_member):
        ring = [(i, (i + s) % n_member) for i in range(n_member)]
        out = lax.dynamic_index_in_dim(mine, (x_at + s) % n_member, 0, keepdims=True)
        got = lax.ppermute(out, "member", ring)
        wanted = lax.dynamic_update_slice_in_dim(wanted, got, (x_at - s) % n_member, 0)

    hi_np, lo_np = dft_tables()
    hi, lo = in_vmem(jnp.asarray(hi_np), jnp.asarray(lo_np))

    first_row = lax.axis_index("lat") * rows
    offset = band_start - first_row - jnp.arange(rows, dtype=jnp.int32) + REACH
    step = jnp.arange(2 * REACH + 1, dtype=jnp.int32)[:, None]
    spread = jnp.zeros((n_basis, 2 * REACH + 1, rows), f32)
    for j in range(band_len):
        spread = spread + jnp.where(offset[None, :] + j == step, band_weights[:, None, :, j], 0.0)
    freq = jnp.asarray(slot_frequencies())
    pick = (jnp.arange(spectra.shape[1], dtype=jnp.int32)[:, None] == freq[None, :]).astype(f32)
    spec = jnp.dot(spectra, pick, precision=lax.Precision.HIGHEST) * slot_scales()[None, :]
    depth = lax.dynamic_slice_in_dim(depth_weights, lax.axis_index("lon") * own_vars, own_vars, 0)
    basis = spread[:, :, None, :] * depth.T[:, None, :, None]

    def coefficients(part):
        flat = part.reshape(n_basis, -1)
        out = lax.dot_general(flat, spec, (((0,), (0,)), ((), ())), precision=lax.Precision.HIGHEST)
        return out.reshape(*part.shape[1:], spec.shape[1])

    inner_coef = coefficients(basis[:, :, :, HALO : rows - HALO])
    edge_coef = coefficients(jnp.concatenate([basis[:, :, :, :HALO], basis[:, :, :, rows - HALO :]], axis=3))
    received, krons, wanted, inner_coef, edge_coef = lax.optimization_barrier(
        (received, krons, wanted, inner_coef, edge_coef)
    )

    up = [(i, i + 1) for i in range(n_lat - 1)]
    down = [(i + 1, i) for i in range(n_lat - 1)]
    top, mid, bot = pl.pallas_call(
        functools.partial(forward_kernel, circles=circles, rows=rows),
        out_shape=(
            pltpu.VMEM((circles, HALO, LENGTH), f32),
            pltpu.VMEM((circles, rows - 2 * HALO, LENGTH), f32),
            pltpu.VMEM((circles, HALO, LENGTH), f32),
        ),
        in_specs=[vmem] * 3,
        out_specs=(vmem, vmem, vmem),
        name="forward",
        compiler_params=GRANT,
    )(*in_vmem(received.reshape(n_lon, circles * rows, tile)), hi, lo)
    before = lax.ppermute(bot, "lat", up)
    after = lax.ppermute(top, "lat", down)
    inner, near = pl.pallas_call(
        functools.partial(inner_kernel, own_vars=own_vars, parts=parts),
        out_shape=(
            pltpu.VMEM((parts - 1, n_lon, 8 * circles, tile), f32),
            pltpu.VMEM((circles, 2 * HALO, LENGTH), f32),
        ),
        in_specs=[vmem] * 6,
        out_specs=(vmem, vmem),
        scratch_shapes=[pltpu.VMEM((8 * (parts - 1) * circles, 256), f32)],
        name="inner",
    compiler_params=GRANT,
    )(*in_vmem(top, mid, bot, inner_coef), hi, lo)
    smooth = pl.pallas_call(
        functools.partial(
            edge_kernel, members=members, own_vars=own_vars, parts=parts, tail=tail
        ),
        out_shape=pltpu.VMEM((parts, n_lon, circles * (8 + tail), tile), f32),
        in_specs=[vmem] * 9,
        out_specs=vmem,
        scratch_shapes=[pltpu.VMEM((circles * (8 + parts * tail), 256), f32)],
        name="edge",
        compiler_params=GRANT,
    )(*in_vmem(top, bot, near, before, after, inner, edge_coef), hi, lo)
    moved = lax.all_to_all(
        smooth.reshape(parts * n_lon, *smooth.shape[2:]),
        ("member", "lon"),
        split_axis=0,
        concat_axis=0,
        tiled=True,
    ).reshape(smooth.shape)

    sizes = dict(members=members, own_vars=own_vars, n_member=n_member, n_lon=n_lon)
    height = variables * (8 + tail)
    total = n_member * members
    scored = pl.pallas_call(
        functools.partial(
            score_kernel, total=total, main=variables * 8, parts=parts, earlier=0, sizes=sizes
        ),
        out_shape=pltpu.VMEM((parts, width, tile), f32),
        in_specs=[vmem] * 6,
        out_specs=vmem,
        scratch_shapes=[pltpu.VMEM((total, height, tile), f32)],
        name="score",
        compiler_params=GRANT,
    )(*in_vmem(moved, *krons, wanted))
    back = lax.all_to_all(scored, "member", split_axis=0, concat_axis=0, tiled=True)
    return pl.pallas_call(
        functools.partial(join_rows_kernel, parts=parts, tail=tail),
        out_shape=shape(target.shape, f32),
        in_specs=[vmem],
        name="join_rows",
        compiler_params=GRANT,
    )(*in_vmem(back))


def solution(mesh):
    in_specs = (
        P("member", None, "lat", "lon"),
        P(),
        P(None, "lat", None),
        P("lat"),
        P(),
        P(),
        P("member", "lat", "lon"),
    )
    out_specs = P("member", "lat", "lon")
    return jax.shard_map(block, mesh=mesh, in_specs=in_specs, out_specs=out_specs, check_vma=False)
```

```python
import functools
import math

import jax
import jax.numpy as jnp
import ml_dtypes
import numpy as np
from jax import lax
from jax.experimental import pallas as pl
from jax.experimental.pallas import tpu as pltpu
from jax.sharding import PartitionSpec as P


PTS = 8
TILE = 128
LENGTH = PTS * TILE
HALO = 8
REACH = 5
GRANT = pltpu.CompilerParams(vmem_limit_bytes=12 << 20)
S2 = math.sqrt(0.5)


def slot_frequencies():
    f1 = np.arange(TILE)
    zero = np.where(f1 <= 64, 8 * f1, 8 * (f1 - 64))
    parts = [zero, 8 * (f1 % 64) + 4]
    for f0 in (1, 2, 3):
        f = 8 * f1 + f0
        parts.append(np.minimum(f, LENGTH - f))
    return np.concatenate(parts).astype(np.int32)


def slot_scales():
    scale = np.full((5 * TILE,), 2.0 / LENGTH)
    scale[0] = 1.0 / LENGTH
    scale[64] = 1.0 / LENGTH
    return scale.astype(np.float32)


def dft_tables():
    r = np.arange(TILE)[:, None]
    f1 = np.arange(TILE)[None, :]

    def ang(f):
        return 2.0 * np.pi * ((r * f) % LENGTH) / LENGTH

    tabs = np.zeros((4, 256, 256))
    low = f1 <= 64
    fz = np.where(low, 8 * f1, 8 * (f1 - 64))
    tabs[0, :TILE, :TILE] = np.where(low, np.cos(ang(fz)), -np.sin(ang(fz)))
    ff = 8 * (f1 % 64) + 4
    tabs[0, TILE:, TILE:] = np.where(f1 < 64, np.cos(ang(ff)), -np.sin(ang(ff)))
    for f0 in (1, 2, 3):
        a = ang(8 * f1 + f0)
        c, s = np.cos(a), np.sin(a)
        tabs[f0, :TILE, :TILE] = c
        tabs[f0, TILE:, :TILE] = s
        tabs[f0, :TILE, TILE:] = -s
        tabs[f0, TILE:, TILE:] = c
    pairs = np.zeros((4, 2, TILE, TILE))
    pairs[0, 0], pairs[0, 1] = tabs[0, :TILE, :TILE], tabs[0, TILE:, TILE:]
    pairs[1:, 0], pairs[1:, 1] = tabs[1:, :TILE, :TILE], tabs[1:, TILE:, :TILE]
    hi = pairs.astype(ml_dtypes.bfloat16)
    lo = (pairs - hi.astype(np.float64)).astype(ml_dtypes.bfloat16)
    return np.stack([hi, lo])


def whole_table(t_ref, level, i):
    a, b = t_ref[level, i, 0], t_ref[level, i, 1]
    if i == 0:
        none = jnp.zeros_like(a)
        upper, lower = (a, none), (none, b)
    else:
        upper, lower = (a, -b), (b, a)
    return jnp.concatenate([jnp.concatenate(upper, axis=1), jnp.concatenate(lower, axis=1)], axis=0)


def split(x):
    hi = x.astype(jnp.bfloat16)
    lo = (x - hi.astype(jnp.float32)).astype(jnp.bfloat16)
    return hi, lo


def mm(a, b):
    return jnp.dot(a, b, preferred_element_type=jnp.float32)


def mm_t(a, b):
    return lax.dot_general(a, b, (((1,), (1,)), ((), ())), preferred_element_type=jnp.float32)


def dot3(x, t_hi, t_lo, op):
    hi, lo = split(x)
    both = op(jnp.concatenate([hi, lo], axis=0), t_hi)
    size = x.shape[0]
    return both[:size] + both[size:] + op(hi, t_lo)


def analyse(x, t_ref, store):
    a = [x[q] + x[q + 4] for q in range(4)]
    b = [x[q] - x[q + 4] for q in range(4)]
    e, g = a[0] + a[2], a[1] + a[3]
    p, m = S2 * (b[1] + b[3]), S2 * (b[1] - b[3])
    pairs = [
        (e + g, e - g),
        (b[0] + m, -p - b[2]),
        (a[0] - a[2], a[3] - a[1]),
        (b[0] - m, b[2] - p),
    ]
    for i, pair in enumerate(pairs):
        store(i, dot3(jnp.concatenate(pair, axis=1), whole_table(t_ref, 0, i), whole_table(t_ref, 1, i), mm))


def forward_kernel(x_ref, t_ref, top_ref, mid_ref, bot_ref, *, circles, rows):
    def store(i, z):
        lanes = slice(256 * i, 256 * (i + 1))
        z = z.reshape(circles, rows, 256)
        top_ref[:, :, lanes] = z[:, :HALO]
        mid_ref[:, :, lanes] = z[:, HALO : rows - HALO]
        bot_ref[:, :, lanes] = z[:, rows - HALO :]

    analyse([x_ref[q] for q in range(PTS)], t_ref, store)


def shifted_sum(ext, coef_ref, c, at, count, lanes):
    acc = None
    for e in range(2 * REACH + 1):
        w = coef_ref[e, c, at : at + count, lanes]
        if w.shape[1] < ext.shape[1]:
            w = jnp.concatenate([w, w], axis=1)
        lead = HALO - REACH + e
        term = w * ext[lead : lead + count]
        acc = term if acc is None else acc + term
    return acc


def coef_lanes(i):
    return slice(0, 256) if i == 0 else slice(TILE * (i + 1), TILE * (i + 2))


def combine(v):
    v0, v4 = v[0][:, :TILE], v[0][:, TILE:]
    v1r, v1i = v[1][:, :TILE], v[1][:, TILE:]
    v2r, v2i = v[2][:, :TILE], v[2][:, TILE:]
    v3r, v3i = v[3][:, :TILE], v[3][:, TILE:]
    s, d = v0 + v4, v0 - v4
    even = [s + v2r, d - v2i, s - v2r, d + v2i]
    dr, si = v1r - v3r, v1i + v3i
    odd = [v1r + v3r, S2 * (dr - si), v3i - v1i, S2 * (-dr - si)]
    return [e + o for e, o in zip(even, odd)] + [e - o for e, o in zip(even, odd)]


def inner_kernel(
    top_ref, mid_ref, bot_ref, coef_ref, t_ref, o_ref, near_ref, y_ref, *, own_vars, parts
):
    circles, count, _ = mid_ref.shape
    near_ref[:, :HALO] = mid_ref[:, :HALO]
    near_ref[:, HALO:] = mid_ref[:, count - HALO :]
    span = 8 * circles
    v = []
    for i in range(4):
        lanes = slice(256 * i, 256 * (i + 1))
        for mc in range(circles):
            ext = jnp.concatenate([top_ref[mc, :, lanes], mid_ref[mc, :, lanes], bot_ref[mc, :, lanes]], axis=0)
            acc = shifted_sum(ext, coef_ref, mc % own_vars, 0, count, coef_lanes(i))
            for p in range(parts - 1):
                y_ref[p * span + 8 * mc : p * span + 8 * mc + 8, :] = acc[8 * p : 8 * p + 8]
        v.append(dot3(y_ref[...], whole_table(t_ref, 0, i), whole_table(t_ref, 1, i), mm_t))
    for q, piece in enumerate(combine(v)):
        for p in range(parts - 1):
            o_ref[p, q] = piece[p * span : (p + 1) * span]


def edge_kernel(
    top_ref, bot_ref, near_ref, up_ref, dn_ref, in_ref, coef_ref, t_ref, o_ref, y_ref, *, members, own_vars, parts, tail
):
    span = 8 * members * own_vars
    main, rest = 8 * own_vars, tail * own_vars
    v = []
    for i in range(4):
        lanes = slice(256 * i, 256 * (i + 1))
        for m in range(members):
            for c in range(own_vars):
                mc = m * own_vars + c
                first = jnp.concatenate([up_ref[mc, :, lanes], top_ref[mc, :, lanes], near_ref[mc, :HALO, lanes]], axis=0)
                final = jnp.concatenate([near_ref[mc, HALO:, lanes], bot_ref[mc, :, lanes], dn_ref[mc, :, lanes]], axis=0)
                y_ref[8 * mc : 8 * mc + 8, :] = shifted_sum(first, coef_ref, c, 0, 8, coef_lanes(i))
                last = shifted_sum(final, coef_ref, c, 8, 8, coef_lanes(i))
                for p in range(parts):
                    lead = span + (p * members + m) * rest + tail * c
                    y_ref[lead : lead + tail, :] = last[tail * p : tail * (p + 1)]
        v.append(dot3(y_ref[...], whole_table(t_ref, 0, i), whole_table(t_ref, 1, i), mm_t))
    for q, piece in enumerate(combine(v)):
        for p in range(parts):
            for m in range(members):
                at = m * (main + rest)
                if p:
                    o_ref[p, q, at : at + main] = in_ref[p - 1, q, m * main : (m + 1) * main]
                else:
                    o_ref[p, q, at : at + main] = piece[m * main : (m + 1) * main]
                lead = span + (p * members + m) * rest
                o_ref[p, q, at + main : at + main + rest] = piece[lead : lead + rest]


def send_kernel(x_ref, o_ref, buf_ref, in_sem, out_sem, *, members, n_lon, own_vars):
    loads, stores = [], []
    for z in range(n_lon):
        for m in range(members):
            loads.append(
                pltpu.make_async_copy(
                    x_ref.at[m, pl.ds(z * own_vars, own_vars)],
                    buf_ref.at[z, pl.ds(m * own_vars, own_vars)],
                    in_sem.at[z * members + m],
                )
            )
        stores.append(pltpu.make_async_copy(buf_ref.at[z], o_ref.at[z], out_sem.at[z]))
    for copy in loads:
        copy.start()
    for z in range(n_lon):
        for m in range(members):
            loads[z * members + m].wait()
        stores[z].start()
    for copy in stores:
        copy.wait()


def mixed(x_ref, k_refs, members, own_vars, n_member, n_lon):
    block = x_ref.shape[2] // members
    main = 8 * own_vars
    k_hi, k_lo, r_hi, r_lo = [ref[...] for ref in k_refs]
    out = []
    for m in range(members):
        lead = m * block
        for j in range(0, n_member, 2):
            pair = range(j, min(j + 2, n_member))
            big = jnp.concatenate([x_ref[i, :, lead : lead + main, :].reshape(n_lon * main, TILE) for i in pair], axis=1)
            small = jnp.concatenate(
                [x_ref[i, :, lead + main : lead + block, :].reshape(n_lon * (block - main), TILE) for i in pair], axis=1
            )
            hi, lo = split(big)
            z = mm(k_hi, hi) + mm(k_hi, lo) + mm(k_lo, hi)
            hi, lo = split(small)
            y = mm(r_hi, hi) + mm(r_hi, lo) + mm(r_lo, hi)
            h = jnp.concatenate([z, y], axis=0)
            h = 0.5 * h * (1.0 + lax.erf(h * S2))
            for i in range(len(pair)):
                out.append(h[:, i * TILE : (i + 1) * TILE])
    return out


def score_kernel(*refs, total, main, parts, earlier, sizes):
    prior = refs[:earlier]
    x_ref, *k_refs, t_ref, o_ref, h_ref = refs[earlier:]
    ready = [(ref, i) for ref in prior for i in range(ref.shape[0])]
    for i, h in enumerate(mixed(x_ref, k_refs, **sizes)):
        h_ref[i] = h
        ready.append((h_ref, i))
    width = main // parts
    rest = t_ref.shape[1] - width
    for p in range(parts):
        for lo, n, at in ((p * width, width, 0), (main + p * rest, rest, width)):
            t = t_ref[p, at : at + n, :]
            h = [ref[i, lo : lo + n, :] for ref, i in ready]
            skill = jnp.abs(h[0] - t)
            for m in range(1, total):
                skill = skill + jnp.abs(h[m] - t)
            spread = None
            for i in range(total):
                for j in range(i):
                    d = jnp.abs(h[i] - h[j])
                    spread = d if spread is None else spread + d
            o_ref[p, at : at + n, :] = skill * (1.0 / total) - spread * (1.0 / (total * total))


def spread_rows(t_ref, o_ref, parts, tail):
    group = t_ref.shape[0]
    for p in range(parts):
        for d in range(group):
            o_ref[p, 8 * d : 8 * d + 8, :] = t_ref[d, 8 * p : 8 * p + 8, :]
            lead = 8 * group + tail * d
            row = 8 * parts + tail * p
            o_ref[p, lead : lead + tail, :] = t_ref[d, row : row + tail, :]


def join_rows_kernel(x_ref, o_ref, *, parts, tail):
    group = o_ref.shape[0]
    for p in range(parts):
        for d in range(group):
            o_ref[d, 8 * p : 8 * p + 8, :] = x_ref[p, 8 * d : 8 * d + 8, :]
            lead = 8 * group + tail * d
            row = 8 * parts + tail * p
            o_ref[d, row : row + tail, :] = x_ref[p, lead : lead + tail, :]


def expand(mix, n):
    size = mix.shape[0]
    span = size * n
    rep = lax.broadcasted_iota(jnp.int32, (span, size), 0) // n == lax.broadcasted_iota(jnp.int32, (span, size), 1)
    rep = rep.astype(jnp.float32).astype(jnp.bfloat16)
    row = lax.broadcasted_iota(jnp.int32, (span, span), 0) % n
    col = lax.broadcasted_iota(jnp.int32, (span, span), 1) % n
    full = []
    for part in split(mix):
        tall = mm(rep, part).astype(jnp.bfloat16)
        full.append(jnp.where(row == col, mm_t(tall, rep), 0.0).astype(jnp.bfloat16))
    return full


def prepare_kernel(mix_ref, t_ref, khi_ref, klo_ref, rhi_ref, rlo_ref, o_ref, *, parts, tail):
    khi_ref[...], klo_ref[...] = expand(mix_ref[...], 8)
    rhi_ref[...], rlo_ref[...] = expand(mix_ref[...], tail)
    spread_rows(t_ref, o_ref, parts, tail)


def in_vmem(*arrays):
    return [pltpu.with_memory_space_constraint(a, pltpu.VMEM) for a in arrays]


def block(fields, spectra, band_weights, band_start, depth_weights, mix_weights, target):
    members, variables, rows, tile = fields.shape
    n_basis = spectra.shape[0]
    band_len = band_weights.shape[2]
    n_member = lax.axis_size("member")
    n_lon = lax.axis_size("lon")
    n_lat = lax.axis_size("lat")
    own_vars = variables // n_lon
    group = variables // n_member
    parts = n_member
    tail = (rows - 8 * parts) // parts
    circles = members * own_vars
    f32 = jnp.float32
    vmem = pl.BlockSpec(memory_space=pltpu.VMEM)
    shape = jax.ShapeDtypeStruct

    hbm = pl.BlockSpec(memory_space=pl.ANY)
    send = pl.pallas_call(
        functools.partial(send_kernel, members=members, n_lon=n_lon, own_vars=own_vars),
        out_shape=shape((n_lon, circles, rows, tile), f32),
        in_specs=[hbm],
        out_specs=hbm,
        scratch_shapes=[
            pltpu.VMEM((n_lon, circles, rows, tile), f32),
            pltpu.SemaphoreType.DMA((members * n_lon,)),
            pltpu.SemaphoreType.DMA((n_lon,)),
        ],
        name="send",
        compiler_params=GRANT,
    )(pltpu.with_memory_space_constraint(fields, pltpu.HBM))
    received = lax.all_to_all(send, "lon", split_axis=0, concat_axis=0, tiled=True)

    width = group * (8 + tail)
    *krons, mine = pl.pallas_call(
        functools.partial(prepare_kernel, parts=parts, tail=tail),
        out_shape=(
            shape((variables * 8, variables * 8), jnp.bfloat16),
            shape((variables * 8, variables * 8), jnp.bfloat16),
            shape((variables * tail, variables * tail), jnp.bfloat16),
            shape((variables * tail, variables * tail), jnp.bfloat16),
            shape((parts, width, tile), f32),
        ),
        name="prepare",
    compiler_params=GRANT,
    )(mix_weights, target)
    x_at = lax.axis_index("member")
    wanted = jnp.zeros((parts, width, tile), f32)
    own = lax.dynamic_index_in_dim(mine, x_at, 0, keepdims=True)
    wanted = lax.dynamic_update_slice_in_dim(wanted, own, x_at, 0)
    for s in range(1, n_member):
        ring = [(i, (i + s) % n_member) for i in range(n_member)]
        out = lax.dynamic_index_in_dim(mine, (x_at + s) % n_member, 0, keepdims=True)
        got = lax.ppermute(out, "member", ring)
        wanted = lax.dynamic_update_slice_in_dim(wanted, got, (x_at - s) % n_member, 0)

    (table,) = in_vmem(jnp.asarray(dft_tables()))

    first_row = lax.axis_index("lat") * rows
    offset = band_start - first_row - jnp.arange(rows, dtype=jnp.int32) + REACH
    step = jnp.arange(2 * REACH + 1, dtype=jnp.int32)[:, None]
    spread = jnp.zeros((n_basis, 2 * REACH + 1, rows), f32)
    for j in range(band_len):
        spread = spread + jnp.where(offset[None, :] + j == step, band_weights[:, None, :, j], 0.0)
    freq = jnp.asarray(slot_frequencies())
    pick = (jnp.arange(spectra.shape[1], dtype=jnp.int32)[:, None] == freq[None, :]).astype(f32)
    spec = jnp.dot(spectra, pick, precision=lax.Precision.HIGHEST) * slot_scales()[None, :]
    depth = lax.dynamic_slice_in_dim(depth_weights, lax.axis_index("lon") * own_vars, own_vars, 0)
    basis = spread[:, :, None, :] * depth.T[:, None, :, None]

    def coefficients(part):
        flat = part.reshape(n_basis, -1)
        out = lax.dot_general(flat, spec, (((0,), (0,)), ((), ())), precision=lax.Precision.HIGHEST)
        return out.reshape(*part.shape[1:], spec.shape[1])

    inner_coef = coefficients(basis[:, :, :, HALO : rows - HALO])
    edge_coef = coefficients(jnp.concatenate([basis[:, :, :, :HALO], basis[:, :, :, rows - HALO :]], axis=3))
    received, krons, wanted, inner_coef, edge_coef = lax.optimization_barrier(
        (received, krons, wanted, inner_coef, edge_coef)
    )

    up = [(i, i + 1) for i in range(n_lat - 1)]
    down = [(i + 1, i) for i in range(n_lat - 1)]
    top, mid, bot = pl.pallas_call(
        functools.partial(forward_kernel, circles=circles, rows=rows),
        out_shape=(
            pltpu.VMEM((circles, HALO, LENGTH), f32),
            pltpu.VMEM((circles, rows - 2 * HALO, LENGTH), f32),
            pltpu.VMEM((circles, HALO, LENGTH), f32),
        ),
        in_specs=[vmem] * 2,
        out_specs=(vmem, vmem, vmem),
        name="forward",
        compiler_params=GRANT,
    )(*in_vmem(received.reshape(n_lon, circles * rows, tile)), table)
    before = lax.ppermute(bot, "lat", up)
    after = lax.ppermute(top, "lat", down)
    inner, near = pl.pallas_call(
        functools.partial(inner_kernel, own_vars=own_vars, parts=parts),
        out_shape=(
            pltpu.VMEM((parts - 1, n_lon, 8 * circles, tile), f32),
            pltpu.VMEM((circles, 2 * HALO, LENGTH), f32),
        ),
        in_specs=[vmem] * 5,
        out_specs=(vmem, vmem),
        scratch_shapes=[pltpu.VMEM((8 * (parts - 1) * circles, 256), f32)],
        name="inner",
    compiler_params=GRANT,
    )(*in_vmem(top, mid, bot, inner_coef), table)
    smooth = pl.pallas_call(
        functools.partial(
            edge_kernel, members=members, own_vars=own_vars, parts=parts, tail=tail
        ),
        out_shape=pltpu.VMEM((parts, n_lon, circles * (8 + tail), tile), f32),
        in_specs=[vmem] * 8,
        out_specs=vmem,
        scratch_shapes=[pltpu.VMEM((circles * (8 + parts * tail), 256), f32)],
        name="edge",
        compiler_params=GRANT,
    )(*in_vmem(top, bot, near, before, after, inner, edge_coef), table)
    moved = lax.all_to_all(
        smooth.reshape(parts * n_lon, *smooth.shape[2:]),
        ("member", "lon"),
        split_axis=0,
        concat_axis=0,
        tiled=True,
    ).reshape(smooth.shape)

    sizes = dict(members=members, own_vars=own_vars, n_member=n_member, n_lon=n_lon)
    height = variables * (8 + tail)
    total = n_member * members
    scored = pl.pallas_call(
        functools.partial(
            score_kernel, total=total, main=variables * 8, parts=parts, earlier=0, sizes=sizes
        ),
        out_shape=pltpu.VMEM((parts, width, tile), f32),
        in_specs=[vmem] * 6,
        out_specs=vmem,
        scratch_shapes=[pltpu.VMEM((total, height, tile), f32)],
        name="score",
        compiler_params=GRANT,
    )(*in_vmem(moved, *krons, wanted))
    back = lax.all_to_all(scored, "member", split_axis=0, concat_axis=0, tiled=True)
    return pl.pallas_call(
        functools.partial(join_rows_kernel, parts=parts, tail=tail),
        out_shape=shape(target.shape, f32),
        in_specs=[vmem],
        name="join_rows",
        compiler_params=GRANT,
    )(*in_vmem(back))


def solution(mesh):
    in_specs = (
        P("member", None, "lat", "lon"),
        P(),
        P(None, "lat", None),
        P("lat"),
        P(),
        P(),
        P("member", "lat", "lon"),
    )
    out_specs = P("member", "lat", "lon")
    return jax.shard_map(block, mesh=mesh, in_specs=in_specs, out_specs=out_specs, check_vma=False)
```
